32 devices in a mesh: seq: 8 (over z, x), head: 4 (over y, core).
Axes of the slice: x: 2, y: 2, z: 4, core: 2. Of those that a mesh axis runs over, the one named last changes fastest.
Arguments:
- query: bfloat16 [8192, 4096], P('seq', 'head'), may hold values from -140 to 140
- key: bfloat16 [8192, 512], P('seq'), may hold values from -7 to 7
- value: bfloat16 [8192, 512], P('seq'), may hold values from -6 to 6
- out_grad: bfloat16 [8192, 4096], P('seq', 'head'), may hold values from -6 to 6
- chosen: int32 [32, 16, 4], P('head', 'seq'), may hold values from 0 to 15, as said below
- drop_seed: int32 [32], P('head'), may hold values from 0 to 16777215
Outputs:
- query_grad: float32 [8192, 4096], P('seq', 'head')
- key_grad: float32 [8192, 512], P(('seq', 'head'))
- value_grad: float32 [8192, 512], P(('seq', 'head'))
The draws below stay inside these ranges and needn't reach their ends.
Inputs may be any that keep to these rules, and one draw needn't show every extreme that they name: `chosen`: for head h and query block b, entry 0 is b; the other entries are distinct blocks before b whose shard lies at most 3 shards of 1024 tokens before the shard of b, or b itself where fewer such blocks exist.
All inputs are finite; a program needn't handle non-finite values.
Results may differ from the reference program's by a relative error of at most 0.014.
Values may be sent and summed in bfloat16 or wider, within the bound.
A program may use at most 128 MiB of HBM per device.

```python
import jax
import jax.numpy as jnp
from jax import lax

HD = 128
HEADS = 32
KVH = 4
BLK = 512
TOPK = 4
TOK_DEV = 1024
WIN = 4
SEQ = 8192
NQB = 16


def key_field(key):
    raw = jnp.clip(jax.random.normal(jax.random.fold_in(key, 11), (SEQ, KVH * HD), jnp.float32), -6.0, 6.0)
    return raw


def draw_key(key, part):
    return key_field(key).astype(jnp.bfloat16)


def draw_query(key, part):
    base = jnp.clip(jax.random.normal(jax.random.fold_in(key, 13), (SEQ, HEADS * HD), jnp.float32), -6.0, 6.0)
    return base.astype(jnp.bfloat16)


def draw_chosen(key, part):
    per_shard = TOK_DEV // BLK
    width = WIN * per_shard
    block_ids = jnp.arange(NQB, dtype=jnp.int32)
    lowest = jnp.maximum(0, (block_ids // per_shard - WIN + 1) * per_shard)
    column = jnp.arange(width, dtype=jnp.int32)
    candidate = lowest[:, None] + column[None, :]
    usable = candidate < block_ids[:, None]
    draws = jax.random.randint(jax.random.fold_in(key, 21), (HEADS, NQB, width), 0, 1 << 20, dtype=jnp.int32)
    scores = jnp.where(usable[None], draws * width + column[None, None, :], -1 - column[None, None, :])
    picked_scores, picked_cols = lax.top_k(scores, TOPK - 1)
    picked = lowest[None, :, None] + picked_cols.astype(jnp.int32)
    picked = jnp.where(picked_scores >= 0, picked, block_ids[None, :, None])
    own = jnp.broadcast_to(block_ids[None, :, None], (HEADS, NQB, 1))
    return jnp.concatenate([own, picked], axis=2).astype(jnp.int32)


def with_ends(drawn, rng, low, high):
    index_at = [jax.random.randint(jax.random.fold_in(rng, axis), (), 0, length) for axis, length in enumerate(drawn.shape)]
    main_axis = drawn.shape.index(max(drawn.shape))
    beside = index_at[:main_axis] + [(index_at[main_axis] + 1) % drawn.shape[main_axis]] + index_at[main_axis + 1:]
    return drawn.at[tuple(index_at)].set(low).at[tuple(beside)].set(high)


def shard_levels(rng, shape, pieces, smallest, high):
    factor_of, own = 1.0, jax.random.fold_in(rng, 6)
    for dim, blocks in pieces:
        steps = jnp.exp(jax.random.uniform(jax.random.fold_in(own, dim), (blocks,), jnp.float32, smallest / len(pieces), high / len(pieces)))
        factor_of = factor_of * jnp.repeat(steps, shape[dim] // blocks).reshape([-1 if axis == dim else 1 for axis in range(len(shape))])
    return factor_of


def normal_values(own_key, extent, scale, most, split=(), held_as=jnp.bfloat16):
    gain = shard_levels(own_key, extent, split, -0.22, 0.18) if split else 1.0
    result = jax.random.normal(own_key, extent, jnp.float32) * scale * gain
    return jnp.minimum(jnp.maximum(result, -most), most).astype(held_as)


def setup_inputs(seed: int = 0) -> dict:
    streams_of = jax.random.split(jax.random.key(seed), 7)
    query = draw_query(jax.random.fold_in(streams_of[6], 71), 0)
    key = draw_key(jax.random.fold_in(streams_of[6], 71), 0)
    value = normal_values(streams_of[2], (SEQ, KVH * HD), 1.0, 6.0, ((0, 8),))
    out_grad = normal_values(streams_of[3], (SEQ, HEADS * HD), 1.0, 6.0, ((0, 8), (1, 4)))
    chosen = draw_chosen(jax.random.fold_in(streams_of[6], 71), 0)
    drop_seed = with_ends(jax.random.randint(streams_of[5], (HEADS,), 0, 16777216), jax.random.fold_in(streams_of[5], 1), 0, 16777215).astype(jnp.int32)
    return dict(query=query, key=key, value=value, out_grad=out_grad, chosen=chosen, drop_seed=drop_seed)


drop_cut = 6554
keep_gain = 1.0 / 0.9


def keep_scale(seed_value, query_pos, key_pos):
    mixed = seed_value + query_pos[:, None] * 40503 + key_pos[None, :] * 9973
    mixed = mixed ^ (jnp.right_shift(mixed, 15) & 131071)
    mixed = mixed * 73244475
    mixed = mixed ^ (jnp.right_shift(mixed, 13) & 524287)
    return jnp.where((mixed & 65535) >= drop_cut, keep_gain, 0.0).astype(jnp.float32)


def block_grads(query_block, out_block, key_sel, value_sel, query_pos, key_pos, allowed, seed_value):
    factor = key_sel.shape[-1] ** -0.5
    scores = jnp.dot(query_block, key_sel.T, preferred_element_type=jnp.float32) * factor
    scores = jnp.where(allowed, scores, -jnp.inf)
    peak = jnp.max(scores, axis=1, keepdims=True)
    total = jnp.sum(jnp.exp(scores - peak), axis=1, keepdims=True)
    probs = jnp.exp(scores - (peak + jnp.log(total)))
    gains = keep_scale(seed_value, query_pos, key_pos)
    dropped = (probs * gains).astype(jnp.bfloat16)
    output = jnp.dot(dropped, value_sel, preferred_element_type=jnp.float32)
    delta = jnp.sum(out_block.astype(jnp.float32) * output, axis=1, keepdims=True)
    pgrad = jnp.dot(out_block, value_sel.T, preferred_element_type=jnp.float32)
    sgrad = (probs * (pgrad * gains - delta)).astype(jnp.bfloat16)
    qgrad = jnp.dot(sgrad, key_sel, preferred_element_type=jnp.float32) * factor
    kgrad = jnp.dot(sgrad.T, query_block, preferred_element_type=jnp.float32) * factor
    vgrad = jnp.dot(dropped.T, out_block, preferred_element_type=jnp.float32)
    return qgrad, kgrad, vgrad


def reference(query, key, value, out_grad, chosen, drop_seed):
    seq_len = query.shape[0]
    blocks = seq_len // BLK
    group = HEADS // KVH
    head_list = jnp.repeat(jnp.arange(HEADS, dtype=jnp.int32), blocks)
    block_list = jnp.tile(jnp.arange(blocks, dtype=jnp.int32), HEADS)
    lists = chosen.reshape(HEADS * blocks, TOPK).astype(jnp.int32)
    seeds = jnp.repeat(drop_seed, blocks).astype(jnp.int32)
    offsets = jnp.arange(BLK, dtype=jnp.int32)

    def visit(carry, item):
        key_grad, value_grad = carry
        head, block, picks, seed_value = item
        kv_col = ((head // group) * HD).astype(jnp.int32)
        query_rows = (block * BLK).astype(jnp.int32)
        query_block = lax.dynamic_slice(query, (query_rows, (head * HD).astype(jnp.int32)), (BLK, HD))
        out_block = lax.dynamic_slice(out_grad, (query_rows, (head * HD).astype(jnp.int32)), (BLK, HD))
        key_parts, value_parts, pos_parts, live_parts = [], [], [], []
        for entry in range(TOPK):
            start = (picks[entry] * BLK).astype(jnp.int32)
            key_parts.append(lax.dynamic_slice(key, (start, kv_col), (BLK, HD)))
            value_parts.append(lax.dynamic_slice(value, (start, kv_col), (BLK, HD)))
            pos_parts.append(start + offsets)
            if entry == 0:
                fresh = jnp.ones((BLK,), dtype=bool)
            else:
                fresh = jnp.broadcast_to(jnp.logical_not(jnp.any(picks[:entry] == picks[entry])), (BLK,))
            live_parts.append(fresh)
        key_pos = jnp.concatenate(pos_parts)
        query_pos = query_rows + offsets
        allowed = (key_pos[None, :] <= query_pos[:, None]) & jnp.concatenate(live_parts)[None, :]
        qgrad, kgrad, vgrad = block_grads(query_block, out_block, jnp.concatenate(key_parts), jnp.concatenate(value_parts), query_pos, key_pos, allowed, seed_value)
        for entry in range(TOPK):
            start = (picks[entry] * BLK).astype(jnp.int32)
            old_key = lax.dynamic_slice(key_grad, (start, kv_col), (BLK, HD))
            key_grad = lax.dynamic_update_slice(key_grad, old_key + kgrad[entry * BLK:(entry + 1) * BLK], (start, kv_col))
            old_value = lax.dynamic_slice(value_grad, (start, kv_col), (BLK, HD))
            value_grad = lax.dynamic_update_slice(value_grad, old_value + vgrad[entry * BLK:(entry + 1) * BLK], (start, kv_col))
        return (key_grad, value_grad), qgrad

    empty = jnp.zeros((seq_len, KVH * HD), jnp.float32)
    (key_grad, value_grad), qgrads = lax.scan(visit, (empty, empty), (head_list, block_list, lists, seeds))
    query_grad = qgrads.reshape(HEADS, blocks, BLK, HD).transpose(1, 2, 0, 3).reshape(seq_len, HEADS * HD)
    return query_grad, key_grad, value_grad
```

```python
import math

import jax
import jax.numpy as jnp
from jax import lax
from jax.experimental import pallas as pl
from jax.experimental.pallas import tpu as pltpu
from jax.sharding import PartitionSpec as P

HD = 128
HEADS = 32
KVH = 4
BLK = 512
TOPK = 4
SPAN = 8
SUB = 128

drop_cut = 6554
keep_gain = 1.0 / 0.9
factor = HD ** (-0.5)
exp_scale = factor * math.log2(math.e)


def shifted(array, axis, by):
    size = lax.axis_size(axis)
    pairs = [(i, i + by) for i in range(size) if 0 <= i + by < size]
    return lax.ppermute(array, axis, pairs)


def kept(x):
    x = x ^ lax.shift_right_logical(x, 15)
    x = x * 73244475
    x = x ^ lax.shift_right_logical(x, 13)
    return (x & 65535) >= drop_cut


def dot(a, b):
    return jnp.dot(a, b, preferred_element_type=jnp.float32)


def grads_kernel(local_blocks, window, steps, chosen_ref, seed_ref, shard_ref, q_ref, do_ref, kv_ref,
                 qg_ref, far_ref, own_ref, s_ref, pg_ref, d_ref, sg_ref, acc_ref, kt_ref, hash_ref):
    step = pl.program_id(0)

    @pl.when(step == 0)
    def _():
        acc_ref[...] = jnp.zeros_like(acc_ref)
        d_ref[0] = jnp.zeros((BLK, BLK), jnp.bfloat16)
        sg_ref[0] = jnp.zeros((BLK, BLK), jnp.bfloat16)
        for slot in range(window):
            kt_ref[slot] = kv_ref[slot, 0].T
        hash_ref[...] = (lax.broadcasted_iota(jnp.int32, (BLK, BLK), 0) * 9973
                         + lax.broadcasted_iota(jnp.int32, (BLK, BLK), 1) * 40503)

    head = step // local_blocks
    block = lax.rem(step, local_blocks)
    shard = shard_ref[0]
    own_block = shard * local_blocks + block
    picks = [chosen_ref[step * TOPK + t] for t in range(TOPK)]
    places = []
    live = [None]
    for t in range(TOPK):
        within = pl.multiple_of(lax.rem(picks[t], local_blocks) * BLK, BLK)
        places.append((shard - picks[t] // local_blocks, within))
        if t:
            dead = picks[t] == picks[0]
            for u in range(1, t):
                dead = jnp.logical_or(dead, picks[t] == picks[u])
            live.append(jnp.logical_not(dead))
    seed_base = seed_ref[head] + own_block * BLK * 40503

    q = q_ref[...]
    do = do_ref[...]
    q_t = q.T
    do_t = do.T
    chunks = [(t, c, (c * SUB if t == 0 else 0)) for t in range(TOPK) for c in range(BLK // SUB)]
    corner = (lax.broadcasted_iota(jnp.int32, (SUB, SUB), 0)
              <= lax.broadcasted_iota(jnp.int32, (SUB, SUB), 1))

    peaks = None
    for t in range(TOPK):
        slot, within = places[t]
        tops = []
        for c in range(BLK // SUB):
            lo = c * SUB if t == 0 else 0
            keys = kv_ref[slot, 0, pl.ds(within + c * SUB, SUB), :]
            s = dot(keys, q_t[:, lo:])
            if t == 0:
                edge = jnp.where(corner, s[:, :SUB], -jnp.inf)
                s = edge if lo + SUB == BLK else jnp.concatenate([edge, s[:, SUB:]], axis=1)
            s_ref[t, c * SUB:(c + 1) * SUB, lo:] = s
            top = jnp.max(s, axis=0, keepdims=True)
            if lo:
                top = jnp.concatenate([jnp.full((1, lo), -jnp.inf, jnp.float32), top], axis=1)
            tops.append(top)
        top = jnp.maximum(jnp.maximum(tops[0], tops[1]), jnp.maximum(tops[2], tops[3]))
        if t:
            top = jnp.where(live[t], top, -jnp.inf)
        peaks = top if peaks is None else jnp.maximum(peaks, top)
    peak = peaks * exp_scale

    total = jnp.zeros((1, BLK), jnp.float32)
    delta = jnp.zeros((1, BLK), jnp.float32)
    for t, c, lo in chunks:
        slot, within = places[t]
        rows = slice(c * SUB, (c + 1) * SUB)
        values = kv_ref[slot, 1, pl.ds(within + c * SUB, SUB), :]
        pg = dot(values, do_t[:, lo:])
        base = peak if t == 0 else jnp.where(live[t], peak, 3e38)
        e = jnp.exp2(s_ref[t, rows, lo:] * exp_scale - base[:, lo:])
        keep = kept(hash_ref[rows, lo:] + (seed_base + picks[t] * BLK * 9973))
        d = jnp.where(keep, e, 0.0)
        pg = jnp.where(keep, pg, 0.0)
        s_ref[t, rows, lo:] = e
        pg_ref[t, rows, lo:] = pg
        d_ref[t, rows, lo:] = d.astype(jnp.bfloat16)
        e_sum = jnp.sum(e, axis=0, keepdims=True)
        dp_sum = jnp.sum(e * pg, axis=0, keepdims=True)
        if lo:
            pad = jnp.zeros((1, lo), jnp.float32)
            e_sum = jnp.concatenate([pad, e_sum], axis=1)
            dp_sum = jnp.concatenate([pad, dp_sum], axis=1)
        total = total + e_sum
        delta = delta + dp_sum

    inv = 1.0 / total
    delta = delta * inv
    q_n = (q_t.astype(jnp.float32) * inv).astype(jnp.bfloat16).T
    do_n = (do_t.astype(jnp.float32) * inv).astype(jnp.bfloat16).T
    qg_t = jnp.zeros((HD, BLK), jnp.float32)
    for t in range(TOPK):
        slot, within = places[t]
        for c in range(BLK // SUB):
            lo = c * SUB if t == 0 else 0
            rows = slice(c * SUB, (c + 1) * SUB)
            sg = s_ref[t, rows, lo:] * (pg_ref[t, rows, lo:] - delta[:, lo:])
            sg_ref[t, rows, lo:] = sg.astype(jnp.bfloat16)
        acc_ref[slot, 1, pl.ds(within, BLK), :] += dot(d_ref[t], do_n)
        acc_ref[slot, 0, pl.ds(within, BLK), :] += dot(sg_ref[t], q_n)
        qg_t = qg_t + dot(kt_ref[slot, :, pl.ds(within, BLK)], sg_ref[t])
    qg_ref[...] = (qg_t * (inv * (keep_gain * factor))).T

    @pl.when(step == steps - 1)
    def _():
        for part, scale in ((0, keep_gain * factor), (1, keep_gain)):
            own_ref[part] = acc_ref[0, part] * scale
            for slot in range(1, window):
                far_ref[slot - 1, part] = (acc_ref[slot, part] * scale).astype(jnp.bfloat16)


def block_grads(query, out_grad, stacked, chosen, drop_seed, shard):
    rows = query.shape[0]
    local_heads = query.shape[1] // HD
    local_blocks = rows // BLK
    window = stacked.shape[0]
    steps = local_heads * local_blocks
    tile = pl.BlockSpec((BLK, HD), lambda i, *_: (lax.rem(i, local_blocks), i // local_blocks))
    flops = steps * TOPK * 5 * 2 * BLK * BLK * HD
    kernel = lambda *refs: grads_kernel(local_blocks, window, steps, *refs)
    return pl.pallas_call(
        kernel,
        name="block_grads",
        grid_spec=pltpu.PrefetchScalarGridSpec(
            num_scalar_prefetch=3,
            grid=(steps,),
            in_specs=[tile, tile, pl.BlockSpec((window, 2, rows, HD), lambda i, *_: (0, 0, 0, 0))],
            out_specs=[
                tile,
                pl.BlockSpec((window - 1, 2, rows, HD), lambda i, *_: (0, 0, 0, 0)),
                pl.BlockSpec((2, rows, HD), lambda i, *_: (0, 0, 0)),
            ],
            scratch_shapes=[
                pltpu.VMEM((TOPK, BLK, BLK), jnp.float32),
                pltpu.VMEM((TOPK, BLK, BLK), jnp.float32),
                pltpu.VMEM((TOPK, BLK, BLK), jnp.bfloat16),
                pltpu.VMEM((TOPK, BLK, BLK), jnp.bfloat16),
                pltpu.VMEM((window, 2, rows, HD), jnp.float32),
                pltpu.VMEM((window, HD, rows), jnp.bfloat16),
                pltpu.VMEM((BLK, BLK), jnp.int32),
            ],
        ),
        out_shape=[
            jax.ShapeDtypeStruct((rows, local_heads * HD), jnp.float32),
            jax.ShapeDtypeStruct((window - 1, 2, rows, HD), jnp.bfloat16),
            jax.ShapeDtypeStruct((2, rows, HD), jnp.float32),
        ],
        compiler_params=pltpu.CompilerParams(vmem_limit_bytes=60 << 20),
        cost_estimate=pl.CostEstimate(flops=flops, bytes_accessed=20 << 20, transcendentals=steps * TOPK * BLK * BLK),
    )(chosen.reshape(-1), drop_seed, shard.reshape(1), query, out_grad, stacked)


def local(query, key, value, out_grad, chosen, drop_seed):
    rows = query.shape[0]
    local_heads = query.shape[1] // HD
    window = min(SPAN, lax.axis_size("seq") // 2)
    shard = lax.axis_index("seq").astype(jnp.int32)
    head_rank = lax.axis_index("head")
    kv_col = head_rank * local_heads // (HEADS // KVH) * HD
    own_pair = jnp.stack(
        [
            lax.dynamic_slice_in_dim(key, kv_col, HD, 1),
            lax.dynamic_slice_in_dim(value, kv_col, HD, 1),
        ]
    )
    stacked = jnp.stack([own_pair] + [shifted(own_pair, "seq", d) for d in range(1, window)])
    query_grad, far, carried = block_grads(query, out_grad, stacked, chosen, drop_seed, shard)
    for d in range(1, window):
        carried = carried + shifted(far[d - 1], "seq", -d).astype(jnp.float32)
    ranks = lax.axis_size("head")
    pieces = carried.reshape(2, ranks, rows // ranks, HD)
    swapped = lax.all_to_all(pieces, "head", 1, 1, tiled=True)
    summed = swapped.reshape(2, KVH, ranks // KVH, rows // ranks, HD).sum(2)
    both = summed.transpose(0, 2, 1, 3).reshape(2, rows // ranks, KVH * HD)
    return (query_grad, both[0], both[1])


def solution(mesh):
    in_specs = (
        P("seq", "head"),
        P("seq", None),
        P("seq", None),
        P("seq", "head"),
        P("head", "seq", None),
        P("head"),
    )
    out_specs = (P("seq", "head"), P(("seq", "head"), None), P(("seq", "head"), None))
    return jax.shard_map(local, mesh=mesh, in_specs=in_specs, out_specs=out_specs, check_vma=False)
```

```python
import math

import jax
import jax.numpy as jnp
from jax import lax
from jax.experimental import pallas as pl
from jax.experimental.pallas import tpu as pltpu
from jax.sharding import PartitionSpec as P

HD = 128
HEADS = 32
KVH = 4
BLK = 512
TOPK = 4
SPAN = 8
SUB = 128

drop_cut = 6554
keep_gain = 1.0 / 0.9
factor = HD ** (-0.5)
exp_scale = factor * math.log2(math.e)


def shifted(array, axis, by):
    size = lax.axis_size(axis)
    pairs = [(i, i + by) for i in range(size) if 0 <= i + by < size]
    return lax.ppermute(array, axis, pairs)


def kept(x):
    x = x ^ lax.shift_right_logical(x, 15)
    x = x * 73244475
    x = x ^ lax.shift_right_logical(x, 13)
    return (x & 65535) >= drop_cut


def dot(a, b):
    return jnp.dot(a, b, preferred_element_type=jnp.float32)


def grads_kernel(local_blocks, window, steps, chosen_ref, seed_ref, place_ref, q_ref, do_ref, key_ref, value_ref,
                 gathered_ref, qg_ref, far_ref, own_ref, s_ref, pg_ref, d_ref, sg_ref, acc_ref, kt_ref, hash_ref, kv_ref,
                 load_sem):
    step = pl.program_id(0)

    @pl.when(step == 0)
    def _():
        col = pl.ds(pl.multiple_of(place_ref[1], HD), HD)
        loads = [
            pltpu.make_async_copy(key_ref.at[:, col], kv_ref.at[0, 0], load_sem.at[0]),
            pltpu.make_async_copy(value_ref.at[:, col], kv_ref.at[0, 1], load_sem.at[1]),
            pltpu.make_async_copy(gathered_ref, kv_ref.at[pl.ds(1, window - 1)], load_sem.at[2]),
        ]
        for load in loads:
            load.start()
        acc_ref[...] = jnp.zeros_like(acc_ref)
        d_ref[0] = jnp.zeros((BLK, BLK), jnp.bfloat16)
        sg_ref[0] = jnp.zeros((BLK, BLK), jnp.bfloat16)
        for load in loads:
            load.wait()
        for slot in range(window):
            kt_ref[slot] = kv_ref[slot, 0].T
        hash_ref[...] = (lax.broadcasted_iota(jnp.int32, (BLK, BLK), 0) * 9973
                         + lax.broadcasted_iota(jnp.int32, (BLK, BLK), 1) * 40503)

    head = step // local_blocks
    block = lax.rem(step, local_blocks)
    shard = place_ref[0]
    own_block = shard * local_blocks + block
    picks = [chosen_ref[step * TOPK + t] for t in range(TOPK)]
    places = []
    live = [None]
    for t in range(TOPK):
        within = pl.multiple_of(lax.rem(picks[t], local_blocks) * BLK, BLK)
        places.append((shard - picks[t] // local_blocks, within))
        if t:
            dead = picks[t] == picks[0]
            for u in range(1, t):
                dead = jnp.logical_or(dead, picks[t] == picks[u])
            live.append(jnp.logical_not(dead))
    seed_base = seed_ref[head] + own_block * BLK * 40503

    q = q_ref[...]
    do = do_ref[...]
    q_t = q.T
    do_t = do.T
    chunks = [(t, c, (c * SUB if t == 0 else 0)) for t in range(TOPK) for c in range(BLK // SUB)]
    corner = (lax.broadcasted_iota(jnp.int32, (SUB, SUB), 0)
              <= lax.broadcasted_iota(jnp.int32, (SUB, SUB), 1))

    peaks = None
    for t in range(TOPK):
        slot, within = places[t]
        tops = []
        for c in range(BLK // SUB):
            lo = c * SUB if t == 0 else 0
            keys = kv_ref[slot, 0, pl.ds(within + c * SUB, SUB), :]
            s = dot(keys, q_t[:, lo:])
            if t == 0:
                edge = jnp.where(corner, s[:, :SUB], -jnp.inf)
                s = edge if lo + SUB == BLK else jnp.concatenate([edge, s[:, SUB:]], axis=1)
            s_ref[t, c * SUB:(c + 1) * SUB, lo:] = s
            top = jnp.max(s, axis=0, keepdims=True)
            if lo:
                top = jnp.concatenate([jnp.full((1, lo), -jnp.inf, jnp.float32), top], axis=1)
            tops.append(top)
        top = jnp.maximum(jnp.maximum(tops[0], tops[1]), jnp.maximum(tops[2], tops[3]))
        if t:
            top = jnp.where(live[t], top, -jnp.inf)
        peaks = top if peaks is None else jnp.maximum(peaks, top)
    peak = peaks * exp_scale

    total = jnp.zeros((1, BLK), jnp.float32)
    delta = jnp.zeros((1, BLK), jnp.float32)
    for t, c, lo in chunks:
        slot, within = places[t]
        rows = slice(c * SUB, (c + 1) * SUB)
        values = kv_ref[slot, 1, pl.ds(within + c * SUB, SUB), :]
        pg = dot(values, do_t[:, lo:])
        base = peak if t == 0 else jnp.where(live[t], peak, 3e38)
        e = jnp.exp2(s_ref[t, rows, lo:] * exp_scale - base[:, lo:])
        keep = kept(hash_ref[rows, lo:] + (seed_base + picks[t] * BLK * 9973))
        d = jnp.where(keep, e, 0.0)
        pg = jnp.where(keep, pg, 0.0)
        s_ref[t, rows, lo:] = e
        pg_ref[t, rows, lo:] = pg
        d_ref[t, rows, lo:] = d.astype(jnp.bfloat16)
        e_sum = jnp.sum(e, axis=0, keepdims=True)
        dp_sum = jnp.sum(e * pg, axis=0, keepdims=True)
        if lo:
            pad = jnp.zeros((1, lo), jnp.float32)
            e_sum = jnp.concatenate([pad, e_sum], axis=1)
            dp_sum = jnp.concatenate([pad, dp_sum], axis=1)
        total = total + e_sum
        delta = delta + dp_sum

    inv = 1.0 / total
    delta = delta * inv
    q_n = (q_t.astype(jnp.float32) * inv).astype(jnp.bfloat16).T
    do_n = (do_t.astype(jnp.float32) * inv).astype(jnp.bfloat16).T
    qg_t = jnp.zeros((HD, BLK), jnp.float32)
    for t in range(TOPK):
        slot, within = places[t]
        for c in range(BLK // SUB):
            lo = c * SUB if t == 0 else 0
            rows = slice(c * SUB, (c + 1) * SUB)
            sg = s_ref[t, rows, lo:] * (pg_ref[t, rows, lo:] - delta[:, lo:])
            sg_ref[t, rows, lo:] = sg.astype(jnp.bfloat16)
        acc_ref[slot, 1, pl.ds(within, BLK), :] += dot(d_ref[t], do_n)
        acc_ref[slot, 0, pl.ds(within, BLK), :] += dot(sg_ref[t], q_n)
        qg_t = qg_t + dot(kt_ref[slot, :, pl.ds(within, BLK)], sg_ref[t])
    qg_ref[...] = (qg_t * (inv * (keep_gain * factor))).T

    @pl.when(step == steps - 1)
    def _():
        for part, scale in ((0, keep_gain * factor), (1, keep_gain)):
            own_ref[part] = acc_ref[0, part] * scale
            for slot in range(1, window):
                far_ref[slot - 1, part] = (acc_ref[slot, part] * scale).astype(jnp.bfloat16)


def block_grads(query, out_grad, key, value, gathered, chosen, drop_seed, place):
    rows = query.shape[0]
    local_heads = query.shape[1] // HD
    local_blocks = rows // BLK
    window = gathered.shape[0] + 1
    steps = local_heads * local_blocks
    tile = pl.BlockSpec((BLK, HD), lambda i, *_: (lax.rem(i, local_blocks), i // local_blocks))
    flops = steps * TOPK * 5 * 2 * BLK * BLK * HD
    kernel = lambda *refs: grads_kernel(local_blocks, window, steps, *refs)
    return pl.pallas_call(
        kernel,
        name="block_grads",
        grid_spec=pltpu.PrefetchScalarGridSpec(
            num_scalar_prefetch=3,
            grid=(steps,),
            in_specs=[tile, tile] + [pl.BlockSpec(memory_space=pl.ANY)] * 3,
            out_specs=[
                tile,
                pl.BlockSpec((window - 1, 2, rows, HD), lambda i, *_: (0, 0, 0, 0)),
                pl.BlockSpec((2, rows, HD), lambda i, *_: (0, 0, 0)),
            ],
            scratch_shapes=[
                pltpu.VMEM((TOPK, BLK, BLK), jnp.float32),
                pltpu.VMEM((TOPK, BLK, BLK), jnp.float32),
                pltpu.VMEM((TOPK, BLK, BLK), jnp.bfloat16),
                pltpu.VMEM((TOPK, BLK, BLK), jnp.bfloat16),
                pltpu.VMEM((window, 2, rows, HD), jnp.float32),
                pltpu.VMEM((window, HD, rows), jnp.bfloat16),
                pltpu.VMEM((BLK, BLK), jnp.int32),
                pltpu.VMEM((window, 2, rows, HD), jnp.bfloat16),
                pltpu.SemaphoreType.DMA((3,)),
            ],
        ),
        out_shape=[
            jax.ShapeDtypeStruct((rows, local_heads * HD), jnp.float32),
            jax.ShapeDtypeStruct((window - 1, 2, rows, HD), jnp.bfloat16),
            jax.ShapeDtypeStruct((2, rows, HD), jnp.float32),
        ],
        compiler_params=pltpu.CompilerParams(vmem_limit_bytes=60 << 20),
        cost_estimate=pl.CostEstimate(flops=flops, bytes_accessed=20 << 20, transcendentals=steps * TOPK * BLK * BLK),
    )(chosen.reshape(-1), drop_seed, place, query, out_grad, key, value, gathered)


CHUNKS = 4


def seq_peer(by):
    size = lax.axis_size("seq")
    return {"seq": lax.rem(lax.axis_index("seq") + by + size, size)}


def meet(peers):
    barrier = pltpu.get_barrier_semaphore()
    for peer in peers:
        pl.semaphore_signal(barrier, inc=1, device_id=peer, device_id_type=pl.DeviceIdType.MESH)
    pl.semaphore_wait(barrier, len(peers))


def remote(src, dst, send, recv, peer):
    return pltpu.make_async_remote_copy(
        src_ref=src, dst_ref=dst, send_sem=send, recv_sem=recv, device_id=peer,
        device_id_type=pl.DeviceIdType.MESH,
    )


def gather_kernel(key_ref, value_ref, far_ref, send_sem, recv_sem):
    shard = lax.axis_index("seq")
    odd = lax.rem(shard, 2)
    col = pl.ds(pl.multiple_of(lax.axis_index("head") * HD, HD), HD)
    half = key_ref.shape[0] // 2
    mate = {"seq": shard + 1 - 2 * odd}
    ahead = seq_peer(2)
    meet([ahead, seq_peer(-2), mate])

    def own(c):
        return (key_ref, value_ref)[c // 2].at[pl.ds(c % 2 * half, half), col]

    def far(k, c):
        return far_ref.at[k, c // 2, pl.ds(c % 2 * half, half), :]

    def own_ahead(c):
        return remote(own(c), far(1, c), send_sem.at[0, c], recv_sem.at[1, c], ahead)

    def own_mate(c):
        return remote(own(c), far(0, c), send_sem.at[1, c], recv_sem.at[0, c], mate)

    def pass_mate(c, k):
        return remote(far(1, c), far(k, c), send_sem.at[2, c], recv_sem.at[k, c], mate)

    def pass_ahead(c):
        return remote(far(0, c), far(2, c), send_sem.at[3, c], recv_sem.at[2, c], ahead)

    for c in range(CHUNKS):
        own_ahead(c).start()

        @pl.when(odd == 0)
        def _():
            own_mate(c).start()

    for c in range(CHUNKS):
        own_ahead(c).wait_recv()

        @pl.when(odd == 0)
        def _():
            pass_mate(c, 2).start()

        @pl.when(odd == 1)
        def _():
            pass_mate(c, 0).start()

        if c:
            @pl.when(odd == 0)
            def _():
                own_mate(c - 1).wait_recv()
                pass_ahead(c - 1).start()

    @pl.when(odd == 0)
    def _():
        own_mate(CHUNKS - 1).wait_recv()
        pass_ahead(CHUNKS - 1).start()
        for c in range(CHUNKS):
            pass_ahead(c).wait_recv()
            own_mate(c).wait_send()
            pass_mate(c, 2).wait_send()
            pass_ahead(c).wait_send()

    @pl.when(odd == 1)
    def _():
        for c in range(CHUNKS):
            own_mate(c).wait_recv()
            pass_ahead(c).wait_recv()
            pass_mate(c, 0).wait_send()

    for c in range(CHUNKS):
        own_ahead(c).wait_send()


def gather(key, value):
    rows = key.shape[0]
    return pl.pallas_call(
        gather_kernel,
        name="gather",
        out_shape=jax.ShapeDtypeStruct((3, 2, rows, HD), jnp.bfloat16),
        in_specs=[pl.BlockSpec(memory_space=pl.ANY)] * 2,
        out_specs=pl.BlockSpec(memory_space=pl.ANY),
        scratch_shapes=[pltpu.SemaphoreType.DMA((4, CHUNKS)), pltpu.SemaphoreType.DMA((3, CHUNKS))],
        compiler_params=pltpu.CompilerParams(collective_id=0, has_side_effects=True),
    )(key, value)


def reduce_kernel(ranks, far_ref, own_ref, kg_ref, vg_ref, in_far, in_near, in_two, in_own, up_near, up_two,
                  in_head, up_head, total, send_sem, recv_sem, head_send, head_recv):
    shard = lax.axis_index("seq")
    rank = lax.axis_index("head")
    odd = lax.rem(shard, 2)
    mate = {"seq": shard + 1 - 2 * odd}
    back = seq_peer(-2)
    others = [{"head": lax.rem(rank + d, ranks)} for d in range(1, ranks)]
    meet([back, seq_peer(2), mate] + others)
    piece = in_near.shape[2]

    def rows(c):
        return pl.ds(c * piece, piece)

    def far_back(c):
        return remote(far_ref.at[2, :, rows(c)], in_far.at[c], send_sem.at[0, c], recv_sem.at[0, c], back)

    def own_mate(c):
        return remote(far_ref.at[0, :, rows(c)], in_own.at[c], send_sem.at[0, c], recv_sem.at[1, c], mate)

    def far_mate(c):
        return remote(far_ref.at[2, :, rows(c)], in_near.at[c], send_sem.at[1, c], recv_sem.at[2, c], mate)

    def near_mate(c):
        return remote(up_near.at[c], in_near.at[c], send_sem.at[1, c], recv_sem.at[2, c], mate)

    def two_back(c):
        return remote(up_two.at[c], in_two.at[c], send_sem.at[2, c], recv_sem.at[3, c], back)

    def to_head(c):
        return remote(up_head.at[c], in_head.at[rank], head_send.at[c], head_recv.at[rank], {"head": c})

    for c in range(ranks):
        @pl.when(odd == 0)
        def _():
            far_back(c).start()

        @pl.when(odd == 1)
        def _():
            far_mate(c).start()

    @pl.when(odd == 1)
    def _():
        for c in range(ranks):
            own_mate(c).start()

    def stage_near(c):
        @pl.when(odd == 0)
        def _():
            far_back(c).wait_recv()
            up_near[c] = (far_ref[0, :, rows(c)].astype(jnp.float32) + in_far[c].astype(jnp.float32)).astype(jnp.bfloat16)
            near_mate(c).start()

    def stage_two(c):
        near_mate(c).wait_recv()
        up_two[c] = (far_ref[1, :, rows(c)].astype(jnp.float32) + in_near[c].astype(jnp.float32)).astype(jnp.bfloat16)
        two_back(c).start()

    def stage_own(c):
        two_back(c).wait_recv()
        total[c] = own_ref[:, rows(c)] + in_two[c].astype(jnp.float32)

        @pl.when(odd == 0)
        def _():
            own_mate(c).wait_recv()
            total[c] += in_own[c].astype(jnp.float32)

        @pl.when(rank == c)
        def _():
            kg_ref[:, c * HD:(c + 1) * HD] = total[c, 0]
            vg_ref[:, c * HD:(c + 1) * HD] = total[c, 1]

        @pl.when(rank != c)
        def _():
            up_head[c] = total[c].astype(jnp.bfloat16)
            to_head(c).start()

    for k in range(ranks + 2):
        if k < ranks:
            stage_near(k)
        if 0 <= k - 1 < ranks:
            stage_two(k - 1)
        if 0 <= k - 2:
            stage_own(k - 2)

    for c in range(ranks):
        @pl.when(rank != c)
        def _():
            remote(up_head.at[c], in_head.at[c], head_send.at[c], head_recv.at[c], {"head": c}).wait_recv()
            kg_ref[:, c * HD:(c + 1) * HD] = in_head[c, 0].astype(jnp.float32)
            vg_ref[:, c * HD:(c + 1) * HD] = in_head[c, 1].astype(jnp.float32)
            to_head(c).wait_send()

        two_back(c).wait_send()

        @pl.when(odd == 0)
        def _():
            far_back(c).wait_send()
            near_mate(c).wait_send()

        @pl.when(odd == 1)
        def _():
            own_mate(c).wait_send()
            far_mate(c).wait_send()


def reduce(far, own):
    ranks = lax.axis_size("head")
    rows = own.shape[1]
    piece = rows // ranks
    part = pltpu.VMEM((ranks, 2, piece, HD), jnp.bfloat16)
    return pl.pallas_call(
        lambda *refs: reduce_kernel(ranks, *refs),
        name="reduce",
        out_shape=[jax.ShapeDtypeStruct((piece, ranks * HD), jnp.float32)] * 2,
        in_specs=[pl.BlockSpec(memory_space=pltpu.VMEM)] * 2,
        out_specs=[pl.BlockSpec(memory_space=pltpu.VMEM)] * 2,
        scratch_shapes=[part] * 8 + [
            pltpu.VMEM((ranks, 2, piece, HD), jnp.float32),
            pltpu.SemaphoreType.DMA((3, ranks)),
            pltpu.SemaphoreType.DMA((4, ranks)),
            pltpu.SemaphoreType.DMA((ranks,)),
            pltpu.SemaphoreType.DMA((ranks,)),
        ],
        compiler_params=pltpu.CompilerParams(collective_id=1, has_side_effects=True, vmem_limit_bytes=32 << 20),
    )(far, own)


def local(query, key, value, out_grad, chosen, drop_seed):
    rows = query.shape[0]
    local_heads = query.shape[1] // HD
    size = lax.axis_size("seq")
    ranks = lax.axis_size("head")
    window = min(SPAN, size // 2)
    kv_col = lax.axis_index("head") * local_heads // (HEADS // KVH) * HD
    place = jnp.stack([lax.axis_index("seq"), kv_col]).astype(jnp.int32)
    paired = window == 4 and ranks == KVH and size % 2 == 0
    if paired:
        gathered = gather(key, value)
    else:
        own_pair = jnp.stack(
            [
                lax.dynamic_slice_in_dim(key, kv_col, HD, 1),
                lax.dynamic_slice_in_dim(value, kv_col, HD, 1),
            ]
        )
        gathered = jnp.stack([shifted(own_pair, "seq", d) for d in range(1, window)])
    query_grad, far, own = block_grads(query, out_grad, key, value, gathered, chosen, drop_seed, place)
    if paired:
        key_grad, value_grad = reduce(far, own)
        return (query_grad, key_grad, value_grad)
    for d in range(1, window):
        own = own + shifted(far[d - 1], "seq", -d).astype(jnp.float32)
    pieces = own.reshape(2, ranks, rows // ranks, HD)
    swapped = lax.all_to_all(pieces, "head", 1, 1, tiled=True)
    summed = swapped.reshape(2, KVH, ranks // KVH, rows // ranks, HD).sum(2)
    both = summed.transpose(0, 2, 1, 3).reshape(2, rows // ranks, KVH * HD)
    return (query_grad, both[0], both[1])


def solution(mesh):
    in_specs = (
        P("seq", "head"),
        P("seq", None),
        P("seq", None),
        P("seq", "head"),
        P("head", "seq", None),
        P("head"),
    )
    out_specs = (P("seq", "head"), P(("seq", "head"), None), P(("seq", "head"), None))
    return jax.shard_map(local, mesh=mesh, in_specs=in_specs, out_specs=out_specs, check_vma=False)
```

```python
import math

import jax
import jax.numpy as jnp
from jax import lax
from jax.experimental import pallas as pl
from jax.experimental.pallas import tpu as pltpu
from jax.sharding import PartitionSpec as P

HD = 128
HEADS = 32
KVH = 4
BLK = 512
TOPK = 4
SPAN = 8
SUB = 128

drop_cut = 6554
keep_gain = 1.0 / 0.9
factor = HD ** (-0.5)
exp_scale = factor * math.log2(math.e)


def shifted(array, axis, by):
    size = lax.axis_size(axis)
    pairs = [(i, i + by) for i in range(size) if 0 <= i + by < size]
    return lax.ppermute(array, axis, pairs)


def kept(x):
    x = x ^ lax.shift_right_logical(x, 15)
    x = x * 73244475
    x = x ^ lax.shift_right_logical(x, 13)
    return (x & 65535) >= drop_cut


def dot(a, b):
    return jnp.dot(a, b, preferred_element_type=jnp.float32)


def grads_kernel(local_blocks, window, steps, chosen_ref, seed_ref, place_ref, q_ref, do_ref, key_ref, value_ref,
                 gathered_ref, qg_ref, far_ref, own_ref, s_ref, pg_ref, d_ref, sg_ref, acc_ref, kt_ref, hash_ref, kv_ref,
                 load_sem):
    step = pl.program_id(0)

    @pl.when(step == 0)
    def _():
        col = pl.ds(pl.multiple_of(place_ref[1], HD), HD)
        loads = [
            pltpu.make_async_copy(key_ref.at[:, col], kv_ref.at[0, 0], load_sem.at[0]),
            pltpu.make_async_copy(value_ref.at[:, col], kv_ref.at[0, 1], load_sem.at[1]),
            pltpu.make_async_copy(gathered_ref, kv_ref.at[pl.ds(1, window - 1)], load_sem.at[2]),
        ]
        for load in loads:
            load.start()
        acc_ref[...] = jnp.zeros_like(acc_ref)
        d_ref[0] = jnp.zeros((BLK, BLK), jnp.bfloat16)
        sg_ref[0] = jnp.zeros((BLK, BLK), jnp.bfloat16)
        for load in loads:
            load.wait()
        for slot in range(window):
            kt_ref[slot] = kv_ref[slot, 0].T
        hash_ref[...] = (lax.broadcasted_iota(jnp.int32, (BLK, BLK), 0) * 9973
                         + lax.broadcasted_iota(jnp.int32, (BLK, BLK), 1) * 40503)

    head = step // local_blocks
    block = lax.rem(step, local_blocks)
    shard = place_ref[0]
    own_block = shard * local_blocks + block
    picks = [chosen_ref[step * TOPK + t] for t in range(TOPK)]
    places = []
    live = [None]
    for t in range(TOPK):
        within = pl.multiple_of(lax.rem(picks[t], local_blocks) * BLK, BLK)
        places.append((shard - picks[t] // local_blocks, within))
        if t:
            dead = picks[t] == picks[0]
            for u in range(1, t):
                dead = jnp.logical_or(dead, picks[t] == picks[u])
            live.append(jnp.logical_not(dead))
    seed_base = seed_ref[head] + own_block * BLK * 40503

    q = q_ref[...]
    do = do_ref[...]
    q_t = q.T
    do_t = do.T
    chunks = [(t, c, (c * SUB if t == 0 else 0)) for t in range(TOPK) for c in range(BLK // SUB)]
    corner = (lax.broadcasted_iota(jnp.int32, (SUB, SUB), 0)
              <= lax.broadcasted_iota(jnp.int32, (SUB, SUB), 1))

    peaks = None
    for t in range(TOPK):
        slot, within = places[t]
        tops = []
        for c in range(BLK // SUB):
            lo = c * SUB if t == 0 else 0
            keys = kv_ref[slot, 0, pl.ds(within + c * SUB, SUB), :]
            s = dot(keys, q_t[:, lo:])
            if t == 0:
                edge = jnp.where(corner, s[:, :SUB], -jnp.inf)
                s = edge if lo + SUB == BLK else jnp.concatenate([edge, s[:, SUB:]], axis=1)
            s_ref[t, c * SUB:(c + 1) * SUB, lo:] = s
            top = jnp.max(s, axis=0, keepdims=True)
            if lo:
                top = jnp.concatenate([jnp.full((1, lo), -jnp.inf, jnp.float32), top], axis=1)
            tops.append(top)
        top = jnp.maximum(jnp.maximum(tops[0], tops[1]), jnp.maximum(tops[2], tops[3]))
        if t:
            top = jnp.where(live[t], top, -jnp.inf)
        peaks = top if peaks is None else jnp.maximum(peaks, top)
    peak = peaks * exp_scale

    total = jnp.zeros((1, BLK), jnp.float32)
    for t, c, lo in chunks:
        slot, within = places[t]
        rows = slice(c * SUB, (c + 1) * SUB)
        base = peak if t == 0 else jnp.where(live[t], peak, 3e38)
        values = kv_ref[slot, 1, pl.ds(within + c * SUB, SUB), :]
        pg_ref[t, rows, lo:] = dot(values, do_t[:, lo:])
        e = jnp.exp2(s_ref[t, rows, lo:] * exp_scale - base[:, lo:])
        s_ref[t, rows, lo:] = e
        e_sum = jnp.sum(e, axis=0, keepdims=True)
        if lo:
            e_sum = jnp.concatenate([jnp.zeros((1, lo), jnp.float32), e_sum], axis=1)
        total = total + e_sum

    inv = 1.0 / total
    q_n = (q_t.astype(jnp.float32) * inv).astype(jnp.bfloat16).T
    do_n = (do_t.astype(jnp.float32) * inv).astype(jnp.bfloat16).T

    def place(t):
        pick = chosen_ref[step * TOPK + t]
        return pick, shard - pick // local_blocks, pl.multiple_of(lax.rem(pick, local_blocks) * BLK, BLK)

    def value_sum(t):
        _, slot, within = place(t)
        acc_ref[slot, 1, pl.ds(within, BLK), :] += dot(d_ref[t], do_n)

    def gate(t, delta, own):
        base = seed_base + place(t)[0] * BLK * 9973
        for c in range(BLK // SUB):
            lo = c * SUB if own else 0
            rows = slice(c * SUB, (c + 1) * SUB)
            e = s_ref[t, rows, lo:]
            keep = kept(hash_ref[rows, lo:] + base)
            d_ref[t, rows, lo:] = jnp.where(keep, e, 0.0).astype(jnp.bfloat16)
            pg = jnp.where(keep, pg_ref[t, rows, lo:], 0.0)
            pg_ref[t, rows, lo:] = pg
            dp_sum = jnp.sum(e * pg, axis=0, keepdims=True)
            if lo:
                dp_sum = jnp.concatenate([jnp.zeros((1, lo), jnp.float32), dp_sum], axis=1)
            delta = delta + dp_sum
        return delta

    def gate_step(t, delta):
        value_sum(t - 1)
        return gate(t, delta, False)

    delta = gate(0, jnp.zeros((1, BLK), jnp.float32), True)
    delta = lax.fori_loop(1, TOPK, gate_step, delta)
    value_sum(TOPK - 1)
    delta = delta * inv
    qg_t = jnp.zeros((HD, BLK), jnp.float32)
    for t in range(TOPK):
        slot, within = places[t]
        for c in range(BLK // SUB):
            lo = c * SUB if t == 0 else 0
            rows = slice(c * SUB, (c + 1) * SUB)
            sg = s_ref[t, rows, lo:] * (pg_ref[t, rows, lo:] - delta[:, lo:])
            sg_ref[t, rows, lo:] = sg.astype(jnp.bfloat16)
        acc_ref[slot, 0, pl.ds(within, BLK), :] += dot(sg_ref[t], q_n)
        qg_t = qg_t + dot(kt_ref[slot, :, pl.ds(within, BLK)], sg_ref[t])
    qg_ref[...] = (qg_t * (inv * (keep_gain * factor))).T

    @pl.when(step == steps - 1)
    def _():
        for part, scale in ((0, keep_gain * factor), (1, keep_gain)):
            own_ref[part] = acc_ref[0, part] * scale
            for slot in range(1, window):
                far_ref[slot - 1, part] = (acc_ref[slot, part] * scale).astype(jnp.bfloat16)


def block_grads(query, out_grad, key, value, gathered, chosen, drop_seed, place):
    rows = query.shape[0]
    local_heads = query.shape[1] // HD
    local_blocks = rows // BLK
    window = gathered.shape[0] + 1
    steps = local_heads * local_blocks
    tile = pl.BlockSpec((BLK, HD), lambda i, *_: (lax.rem(i, local_blocks), i // local_blocks))
    flops = steps * TOPK * 5 * 2 * BLK * BLK * HD
    kernel = lambda *refs: grads_kernel(local_blocks, window, steps, *refs)
    return pl.pallas_call(
        kernel,
        name="block_grads",
        grid_spec=pltpu.PrefetchScalarGridSpec(
            num_scalar_prefetch=3,
            grid=(steps,),
            in_specs=[tile, tile] + [pl.BlockSpec(memory_space=pl.ANY)] * 3,
            out_specs=[
                tile,
                pl.BlockSpec((window - 1, 2, rows, HD), lambda i, *_: (0, 0, 0, 0)),
                pl.BlockSpec((2, rows, HD), lambda i, *_: (0, 0, 0)),
            ],
            scratch_shapes=[
                pltpu.VMEM((TOPK, BLK, BLK), jnp.float32),
                pltpu.VMEM((TOPK, BLK, BLK), jnp.float32),
                pltpu.VMEM((TOPK, BLK, BLK), jnp.bfloat16),
                pltpu.VMEM((TOPK, BLK, BLK), jnp.bfloat16),
                pltpu.VMEM((window, 2, rows, HD), jnp.float32),
                pltpu.VMEM((window, HD, rows), jnp.bfloat16),
                pltpu.VMEM((BLK, BLK), jnp.int32),
                pltpu.VMEM((window, 2, rows, HD), jnp.bfloat16),
                pltpu.SemaphoreType.DMA((3,)),
            ],
        ),
        out_shape=[
            jax.ShapeDtypeStruct((rows, local_heads * HD), jnp.float32),
            jax.ShapeDtypeStruct((window - 1, 2, rows, HD), jnp.bfloat16),
            jax.ShapeDtypeStruct((2, rows, HD), jnp.float32),
        ],
        compiler_params=pltpu.CompilerParams(vmem_limit_bytes=60 << 20),
        cost_estimate=pl.CostEstimate(flops=flops, bytes_accessed=20 << 20, transcendentals=steps * TOPK * BLK * BLK),
    )(chosen.reshape(-1), drop_seed, place, query, out_grad, key, value, gathered)


CHUNKS = 4


def seq_peer(by):
    size = lax.axis_size("seq")
    return {"seq": lax.rem(lax.axis_index("seq") + by + size, size)}


def meet(peers):
    barrier = pltpu.get_barrier_semaphore()
    for peer in peers:
        pl.semaphore_signal(barrier, inc=1, device_id=peer, device_id_type=pl.DeviceIdType.MESH)
    pl.semaphore_wait(barrier, len(peers))


def remote(src, dst, send, recv, peer):
    return pltpu.make_async_remote_copy(
        src_ref=src, dst_ref=dst, send_sem=send, recv_sem=recv, device_id=peer,
        device_id_type=pl.DeviceIdType.MESH,
    )


def gather_kernel(key_ref, value_ref, far_ref, send_sem, recv_sem):
    shard = lax.axis_index("seq")
    odd = lax.rem(shard, 2)
    col = pl.ds(pl.multiple_of(lax.axis_index("head") * HD, HD), HD)
    half = key_ref.shape[0] // 2
    mate = {"seq": shard + 1 - 2 * odd}
    ahead = seq_peer(2)
    meet([ahead, seq_peer(-2), mate])

    def own(c):
        return (key_ref, value_ref)[c // 2].at[pl.ds(c % 2 * half, half), col]

    def far(k, c):
        return far_ref.at[k, c // 2, pl.ds(c % 2 * half, half), :]

    def own_ahead(c):
        return remote(own(c), far(1, c), send_sem.at[0, c], recv_sem.at[1, c], ahead)

    def own_mate(c):
        return remote(own(c), far(0, c), send_sem.at[1, c], recv_sem.at[0, c], mate)

    def pass_mate(c, k):
        return remote(far(1, c), far(k, c), send_sem.at[2, c], recv_sem.at[k, c], mate)

    def pass_ahead(c):
        return remote(far(0, c), far(2, c), send_sem.at[3, c], recv_sem.at[2, c], ahead)

    for c in range(CHUNKS):
        own_ahead(c).start()

        @pl.when(odd == 0)
        def _():
            own_mate(c).start()

    for c in range(CHUNKS):
        own_ahead(c).wait_recv()

        @pl.when(odd == 0)
        def _():
            pass_mate(c, 2).start()

        @pl.when(odd == 1)
        def _():
            pass_mate(c, 0).start()

        if c:
            @pl.when(odd == 0)
            def _():
                own_mate(c - 1).wait_recv()
                pass_ahead(c - 1).start()

    @pl.when(odd == 0)
    def _():
        own_mate(CHUNKS - 1).wait_recv()
        pass_ahead(CHUNKS - 1).start()
        for c in range(CHUNKS):
            pass_ahead(c).wait_recv()
            own_mate(c).wait_send()
            pass_mate(c, 2).wait_send()
            pass_ahead(c).wait_send()

    @pl.when(odd == 1)
    def _():
        for c in range(CHUNKS):
            own_mate(c).wait_recv()
            pass_ahead(c).wait_recv()
            pass_mate(c, 0).wait_send()

    for c in range(CHUNKS):
        own_ahead(c).wait_send()


def gather(key, value):
    rows = key.shape[0]
    return pl.pallas_call(
        gather_kernel,
        name="gather",
        out_shape=jax.ShapeDtypeStruct((3, 2, rows, HD), jnp.bfloat16),
        in_specs=[pl.BlockSpec(memory_space=pl.ANY)] * 2,
        out_specs=pl.BlockSpec(memory_space=pl.ANY),
        scratch_shapes=[pltpu.SemaphoreType.DMA((4, CHUNKS)), pltpu.SemaphoreType.DMA((3, CHUNKS))],
        compiler_params=pltpu.CompilerParams(collective_id=0, has_side_effects=True),
    )(key, value)


def reduce_kernel(ranks, far_ref, own_ref, kg_ref, vg_ref, in_far, in_near, in_two, in_own, up_near, up_two,
                  in_head, up_head, total, send_sem, recv_sem, head_send, head_recv):
    shard = lax.axis_index("seq")
    rank = lax.axis_index("head")
    odd = lax.rem(shard, 2)
    mate = {"seq": shard + 1 - 2 * odd}
    back = seq_peer(-2)
    others = [{"head": lax.rem(rank + d, ranks)} for d in range(1, ranks)]
    meet([back, seq_peer(2), mate] + others)
    piece = in_near.shape[2]

    def rows(c):
        return pl.ds(c * piece, piece)

    def far_back(c):
        return remote(far_ref.at[2, :, rows(c)], in_far.at[c], send_sem.at[0, c], recv_sem.at[0, c], back)

    def own_mate(c):
        return remote(far_ref.at[0, :, rows(c)], in_own.at[c], send_sem.at[0, c], recv_sem.at[1, c], mate)

    def far_mate(c):
        return remote(far_ref.at[2, :, rows(c)], in_near.at[c], send_sem.at[1, c], recv_sem.at[2, c], mate)

    def near_mate(c):
        return remote(up_near.at[c], in_near.at[c], send_sem.at[1, c], recv_sem.at[2, c], mate)

    def two_back(c):
        return remote(up_two.at[c], in_two.at[c], send_sem.at[2, c], recv_sem.at[3, c], back)

    def to_head(c):
        return remote(up_head.at[c], in_head.at[rank], head_send.at[c], head_recv.at[rank], {"head": c})

    for c in range(ranks):
        @pl.when(odd == 0)
        def _():
            far_back(c).start()

        @pl.when(odd == 1)
        def _():
            far_mate(c).start()

    @pl.when(odd == 1)
    def _():
        for c in range(ranks):
            own_mate(c).start()

    def stage_near(c):
        @pl.when(odd == 0)
        def _():
            far_back(c).wait_recv()
            up_near[c] = (far_ref[0, :, rows(c)].astype(jnp.float32) + in_far[c].astype(jnp.float32)).astype(jnp.bfloat16)
            near_mate(c).start()

    def stage_two(c):
        near_mate(c).wait_recv()
        up_two[c] = (far_ref[1, :, rows(c)].astype(jnp.float32) + in_near[c].astype(jnp.float32)).astype(jnp.bfloat16)
        two_back(c).start()

    def stage_own(c):
        two_back(c).wait_recv()
        total[c] = own_ref[:, rows(c)] + in_two[c].astype(jnp.float32)

        @pl.when(odd == 0)
        def _():
            own_mate(c).wait_recv()
            total[c] += in_own[c].astype(jnp.float32)

        @pl.when(rank == c)
        def _():
            kg_ref[:, c * HD:(c + 1) * HD] = total[c, 0]
            vg_ref[:, c * HD:(c + 1) * HD] = total[c, 1]

        @pl.when(rank != c)
        def _():
            up_head[c] = total[c].astype(jnp.bfloat16)
            to_head(c).start()

    for k in range(ranks + 2):
        if k < ranks:
            stage_near(k)
        if 0 <= k - 1 < ranks:
            stage_two(k - 1)
        if 0 <= k - 2:
            stage_own(k - 2)

    for c in range(ranks):
        @pl.when(rank != c)
        def _():
            remote(up_head.at[c], in_head.at[c], head_send.at[c], head_recv.at[c], {"head": c}).wait_recv()
            kg_ref[:, c * HD:(c + 1) * HD] = in_head[c, 0].astype(jnp.float32)
            vg_ref[:, c * HD:(c + 1) * HD] = in_head[c, 1].astype(jnp.float32)
            to_head(c).wait_send()

        two_back(c).wait_send()

        @pl.when(odd == 0)
        def _():
            far_back(c).wait_send()
            near_mate(c).wait_send()

        @pl.when(odd == 1)
        def _():
            own_mate(c).wait_send()
            far_mate(c).wait_send()


def reduce(far, own):
    ranks = lax.axis_size("head")
    rows = own.shape[1]
    piece = rows // ranks
    part = pltpu.VMEM((ranks, 2, piece, HD), jnp.bfloat16)
    return pl.pallas_call(
        lambda *refs: reduce_kernel(ranks, *refs),
        name="reduce",
        out_shape=[jax.ShapeDtypeStruct((piece, ranks * HD), jnp.float32)] * 2,
        in_specs=[pl.BlockSpec(memory_space=pltpu.VMEM)] * 2,
        out_specs=[pl.BlockSpec(memory_space=pltpu.VMEM)] * 2,
        scratch_shapes=[part] * 8 + [
            pltpu.VMEM((ranks, 2, piece, HD), jnp.float32),
            pltpu.SemaphoreType.DMA((3, ranks)),
            pltpu.SemaphoreType.DMA((4, ranks)),
            pltpu.SemaphoreType.DMA((ranks,)),
            pltpu.SemaphoreType.DMA((ranks,)),
        ],
        compiler_params=pltpu.CompilerParams(collective_id=1, has_side_effects=True, vmem_limit_bytes=32 << 20),
    )(far, own)


def local(query, key, value, out_grad, chosen, drop_seed):
    rows = query.shape[0]
    local_heads = query.shape[1] // HD
    size = lax.axis_size("seq")
    ranks = lax.axis_size("head")
    window = min(SPAN, size // 2)
    kv_col = lax.axis_index("head") * local_heads // (HEADS // KVH) * HD
    place = jnp.stack([lax.axis_index("seq"), kv_col]).astype(jnp.int32)
    paired = window == 4 and ranks == KVH and size % 2 == 0
    if paired:
        gathered = gather(key, value)
    else:
        own_pair = jnp.stack(
            [
                lax.dynamic_slice_in_dim(key, kv_col, HD, 1),
                lax.dynamic_slice_in_dim(value, kv_col, HD, 1),
            ]
        )
        gathered = jnp.stack([shifted(own_pair, "seq", d) for d in range(1, window)])
    query_grad, far, own = block_grads(query, out_grad, key, value, gathered, chosen, drop_seed, place)
    if paired:
        key_grad, value_grad = reduce(far, own)
        return (query_grad, key_grad, value_grad)
    for d in range(1, window):
        own = own + shifted(far[d - 1], "seq", -d).astype(jnp.float32)
    pieces = own.reshape(2, ranks, rows // ranks, HD)
    swapped = lax.all_to_all(pieces, "head", 1, 1, tiled=True)
    summed = swapped.reshape(2, KVH, ranks // KVH, rows // ranks, HD).sum(2)
    both = summed.transpose(0, 2, 1, 3).reshape(2, rows // ranks, KVH * HD)
    return (query_grad, both[0], both[1])


def solution(mesh):
    in_specs = (
        P("seq", "head"),
        P("seq", None),
        P("seq", None),
        P("seq", "head"),
        P("head", "seq", None),
        P("head"),
    )
    out_specs = (P("seq", "head"), P(("seq", "head"), None), P(("seq", "head"), None))
    return jax.shard_map(local, mesh=mesh, in_specs=in_specs, out_specs=out_specs, check_vma=False)
```
